32 devices in a mesh: groups: 2 (over y), ctx: 4 (over z), head: 2 (over x), sub: 2 (over core).
Axes of the slice: x: 2, y: 2, z: 4, core: 2. Of those that a mesh axis runs over, the one named last changes fastest.
Arguments:
- hidden_in: bfloat16 [1024, 5120], P(('groups', 'ctx'), 'sub'), parts along dimension 0, may hold values from -6 to 6
- w_qkv: bfloat16 [5120, 8, 896], P('sub', 'head', 'ctx'), may hold values from -0.078125 to 0.078125
- qkv_bias: bfloat16 [8, 896], P('head'), may hold values from -3 to 3
- w_out: bfloat16 [8, 640, 5120], P('head', 'ctx'), may hold values from -0.078125 to 0.078125
- prev_keys: bfloat16 [1024, 8, 128], P(('groups', 'ctx', 'sub'), 'head'), parts along dimension 0, may hold values from -60 to 60
- prev_values: bfloat16 [1024, 8, 128], P(('groups', 'ctx', 'sub'), 'head'), parts along dimension 0, may hold values from -6 to 6
- shard_blocks: int32 [8], P('groups'), parts along dimension 0, may hold values from 0 to 3, each once
Outputs:
- attn_out: bfloat16 [1024, 5120], P(('groups', 'ctx', 'sub'), 'head'), parts along dimension 0
The draws below stay inside these ranges and needn't reach their ends.
There are 2 independent parts, one for each index of `groups`. The reference program is written for one: setup_inputs(seed, part) draws one part's arguments, and reference() takes and returns one part's arrays. A program takes and returns all parts, laid end to end along the dimension named above; an argument that names none is the same for every part. Nothing has to cross between parts.
Inputs may be any that keep to these rules, and one draw needn't show every extreme that they name: Index c of ctx holds the positions shard_blocks[c] * 128 to shard_blocks[c] * 128 + 127; every block occurs once.
All inputs are finite; a program needn't handle non-finite values.
Results may differ from the reference program's by a relative error of at most 0.015.
The reference program's roundings to bfloat16 on the way (of `head_out`) count: a program that leaves them out, or rounds other values in their place, can miss the bound.
Values may be sent and summed in bfloat16 or wider, within the bound.
No kernel may reach another device: no remote copies, remote signals or barrier semaphores. Data moves between devices by JAX's collectives and lax.ppermute only.
A program may use at most 64 MiB of HBM per device.

```python
import jax
import jax.numpy as jnp
from jax import lax

D = 5120
KVH = 8
G = 5
HD = 128
TOK_CTX = 128
NPREV = 2
CH = 256
TOKENS = 512
N_CTX = 4
N_HEAD = 2


def draw_prev_keys(key, part):
    row_count = NPREV * CH
    drawn = jax.random.normal(key, (row_count, KVH, HD), jnp.float32)
    return jnp.clip(drawn, -60.0, 60.0).astype(jnp.bfloat16)


def steps_of(rng, dims, shards, smallest, high):
    level = 1.0
    for position, shards_of in shards:
        heights = jax.random.uniform(jax.random.fold_in(jax.random.fold_in(rng, 6), position), (shards_of,), jnp.float32, smallest / len(shards), high / len(shards))
        level = level * jnp.repeat(jnp.exp(heights), dims[position] // shards_of).reshape((-1,) + (1,) * (len(dims) - 1 - position))
    return level


def bell_draw(own_key, extent, scale, bound, shards=(), kind=jnp.bfloat16):
    array = scale * jax.random.normal(own_key, extent, jnp.float32)
    if shards:
        array = array * steps_of(own_key, extent, shards, -0.22, 0.18)
    return jnp.clip(array, -bound, bound).astype(kind)


def setup_inputs(seed: int = 0, part: int = 0) -> dict:
    splits = jax.random.split(jax.random.key(seed), 8)
    own_keys = jax.random.split(jax.random.fold_in(splits[7], part), 8)
    return {
        "hidden_in": bell_draw(own_keys[0], (TOKENS, D), 1.0, 6.0, ((0, 4), (1, 2))),
        "w_qkv": bell_draw(splits[1], (D, KVH, (G + 2) * HD), D ** -0.5, 0.078125, ((0, 2), (1, 2), (2, 4))),
        "qkv_bias": bell_draw(splits[2], (KVH, (G + 2) * HD), 0.5, 3.0, ((0, 2),)),
        "w_out": bell_draw(splits[3], (KVH, G * HD, D), (KVH * G * HD) ** -0.5, 0.078125, ((0, 2), (1, 4))),
        "prev_keys": draw_prev_keys(jax.random.fold_in(jax.random.fold_in(splits[7], part), 71), part),
        "prev_values": bell_draw(own_keys[5], (NPREV * CH, KVH, HD), 1.0, 6.0, ((0, 8), (1, 2))),
        "shard_blocks": jax.random.permutation(own_keys[6], N_CTX).astype(jnp.int32),
    }


rope_base = 10000000.0
neg_big = -1e30


def rotate(vectors, positions):
    half_width = vectors.shape[-1] // 2
    frequency = rope_base ** (-(jnp.arange(half_width, dtype=jnp.float32) * 2.0) / vectors.shape[-1])
    angles = positions.astype(jnp.float32)[:, None] * frequency[None, :]
    extra = (1,) * (vectors.ndim - 2)
    cosine = jnp.cos(angles).reshape((angles.shape[0],) + extra + (half_width,))
    sine_part = jnp.sin(angles).reshape((angles.shape[0],) + extra + (half_width,))
    first = vectors[..., :half_width]
    second = vectors[..., half_width:]
    return jnp.concatenate([first * cosine - second * sine_part, second * cosine + first * sine_part], axis=-1)


def attend(q_intra, q_succ, q_inter, span_row, local_row, cur_keys, cur_values, cur_span, cur_local, old_keys, old_values, old_span):
    row_count = q_intra.shape[0] * G
    score_scale = HD ** -0.5
    flat_intra = q_intra.reshape(row_count, HD)
    flat_succ = q_succ.reshape(row_count, HD)
    flat_inter = q_inter.reshape(row_count, HD)
    span_rep = jnp.repeat(span_row, G)
    local_rep = jnp.repeat(local_row, G)
    s_intra = jnp.dot(flat_intra, cur_keys.T, preferred_element_type=jnp.float32) * score_scale
    s_succ = jnp.dot(flat_succ, cur_keys.T, preferred_element_type=jnp.float32) * score_scale
    same_span = cur_span[None, :] == span_rep[:, None]
    before = cur_span[None, :] == span_rep[:, None] - 1
    allowed = (same_span & (cur_local[None, :] <= local_rep[:, None])) | before
    s_cur = jnp.where(same_span, s_intra, s_succ)
    o_succ = jnp.dot(flat_succ, old_keys.T, preferred_element_type=jnp.float32) * score_scale
    o_inter = jnp.dot(flat_inter, old_keys.T, preferred_element_type=jnp.float32) * score_scale
    s_old = jnp.where(old_span[None, :] == span_rep[:, None] - 1, o_succ, o_inter)
    running_max = jnp.maximum(jnp.max(jnp.where(allowed, s_cur, neg_big), axis=1), jnp.max(s_old, axis=1))
    w_cur = jnp.where(allowed, jnp.exp(s_cur - running_max[:, None]), 0.0)
    w_old = jnp.exp(s_old - running_max[:, None])
    weight_sum = jnp.sum(w_cur, axis=1) + jnp.sum(w_old, axis=1)
    weighted = jnp.dot(w_cur.astype(jnp.bfloat16), cur_values, preferred_element_type=jnp.float32)
    weighted = weighted + jnp.dot(w_old.astype(jnp.bfloat16), old_values, preferred_element_type=jnp.float32)
    head_out = (weighted / weight_sum[:, None]).astype(jnp.bfloat16)
    return head_out.reshape(q_intra.shape[0], G * HD)


def reference(hidden_in, w_qkv, qkv_bias, w_out, prev_keys, prev_values, shard_blocks):
    row_ids = jnp.arange(TOKENS, dtype=jnp.int32)
    owner = shard_blocks[row_ids // TOK_CTX]
    positions = owner * TOK_CTX + row_ids % TOK_CTX
    span_ids = NPREV + positions // CH
    local_pos = positions % CH
    joined = jnp.dot(hidden_in, w_qkv.reshape(D, KVH * (G + 2) * HD), preferred_element_type=jnp.float32)
    joined = joined.reshape(TOKENS, KVH, G + 2, HD) + qkv_bias.astype(jnp.float32).reshape(KVH, G + 2, HD)
    queries = joined[:, :, :G]
    q_intra = rotate(queries, local_pos).astype(jnp.bfloat16)
    q_succ = rotate(queries, local_pos + CH).astype(jnp.bfloat16)
    q_inter = rotate(queries, jnp.full((TOKENS,), 2 * CH - 1, jnp.int32)).astype(jnp.bfloat16)
    cur_keys = rotate(joined[:, :, G], local_pos).astype(jnp.bfloat16)
    cur_values = joined[:, :, G + 1].astype(jnp.bfloat16)
    old_rows = jnp.arange(NPREV * CH, dtype=jnp.int32)
    old_keys = rotate(prev_keys.astype(jnp.float32), old_rows % CH).astype(jnp.bfloat16)
    old_span = old_rows // CH

    def per_head(head_index):
        key_now = lax.dynamic_index_in_dim(cur_keys, head_index, 1, keepdims=False)
        value_now = lax.dynamic_index_in_dim(cur_values, head_index, 1, keepdims=False)
        key_old = lax.dynamic_index_in_dim(old_keys, head_index, 1, keepdims=False)
        value_old = lax.dynamic_index_in_dim(prev_values, head_index, 1, keepdims=False)
        intra_head = lax.dynamic_index_in_dim(q_intra, head_index, 1, keepdims=False)
        succ_head = lax.dynamic_index_in_dim(q_succ, head_index, 1, keepdims=False)
        inter_head = lax.dynamic_index_in_dim(q_inter, head_index, 1, keepdims=False)

        def per_block(block_index):
            first_row = (block_index * TOK_CTX).astype(jnp.int32)

            def take(values):
                return lax.dynamic_slice_in_dim(values, first_row, TOK_CTX, 0)

            return attend(take(intra_head), take(succ_head), take(inter_head), take(span_ids), take(local_pos),
                          key_now, value_now, span_ids, local_pos, key_old, value_old, old_span)

        return lax.map(per_block, jnp.arange(N_CTX, dtype=jnp.int32))

    attended = lax.map(per_head, jnp.arange(KVH, dtype=jnp.int32))
    attended = jnp.transpose(attended, (1, 2, 0, 3)).reshape(TOKENS, KVH * G * HD)
    group_rows = (KVH // N_HEAD) * G * HD
    w_flat = w_out.reshape(KVH * G * HD, D)
    result = jnp.zeros((TOKENS, D), jnp.float32)
    for group in range(N_HEAD):
        term = jnp.dot(attended[:, group * group_rows:(group + 1) * group_rows],
                       w_flat[group * group_rows:(group + 1) * group_rows], preferred_element_type=jnp.float32)
        result = result + lax.optimization_barrier(term.astype(jnp.bfloat16)).astype(jnp.float32)
    return result.astype(jnp.bfloat16)
```

```python
import functools
import math

import jax
import jax.numpy as jnp
from jax import lax
from jax.experimental import pallas as pl
from jax.experimental.pallas import tpu as pltpu
from jax.sharding import PartitionSpec as P

G = 5
HD = 128
NPREV = 2


rope_base = 10000000.0
neg_big = -1e30


def rotate(vectors, positions):
    half_width = vectors.shape[-1] // 2
    frequency = rope_base ** (
        -(jnp.arange(half_width, dtype=jnp.float32) * 2.0) / vectors.shape[-1]
    )
    angles = positions.astype(jnp.float32)[:, None] * frequency[None, :]
    extra = (1,) * (vectors.ndim - 2)
    cosine = jnp.cos(angles).reshape((angles.shape[0],) + extra + (half_width,))
    sine_part = jnp.sin(angles).reshape((angles.shape[0],) + extra + (half_width,))
    first = vectors[..., :half_width]
    second = vectors[..., half_width:]
    return jnp.concatenate(
        [first * cosine - second * sine_part, second * cosine + first * sine_part], axis=-1
    )


def lookup(small_table, wanted):
    entries = jnp.arange(small_table.shape[0], dtype=jnp.int32)
    return jnp.sum(jnp.where(wanted[..., None] == entries, small_table, 0), axis=-1)


def flip(value, axis, k):
    return lax.ppermute(value, axis, [(i, i ^ k) for i in range(lax.axis_size(axis))])


def dot32(a, b, dims):
    return lax.dot_general(a, b, (dims, ((), ())), preferred_element_type=jnp.float32)


vmem = pl.BlockSpec(memory_space=pltpu.VMEM)


def project_kernel(n_ctx, rows, scal, x_ref, *refs):
    mine, theirs = refs[: n_ctx - 1], refs[n_ctx - 1 : 2 * n_ctx - 2]
    w_ref, send_ref, own_ref, xs = refs[2 * n_ctx - 2 :]
    me_sub, slot = scal[0], scal[1]

    @pl.when(pl.program_id(0) == 0)
    def _():
        for k in range(n_ctx):
            at = pl.ds(pl.multiple_of(scal[2 + k] * rows, rows), rows)
            if k == 0:
                for t in range(2):
                    here = jnp.where(me_sub == t, 0, 1)
                    xs[here, at, :] = x_ref[t * rows : (t + 1) * rows, :]
            else:
                xs[slot, at, :] = mine[k - 1][...]
                xs[1 - slot, at, :] = theirs[k - 1][...]

    w = w_ref[0]
    send_ref[0] = dot32(w, xs[1], ((1,), (1,))).astype(jnp.bfloat16)
    own_ref[0] = dot32(w, xs[0], ((1,), (1,)))


def project(scal, x, mine, theirs, w_t):
    n_ctx, cols, feats = w_t.shape
    rows = x.shape[0] // 2
    total = n_ctx * rows
    return pl.pallas_call(
        functools.partial(project_kernel, n_ctx, rows),
        grid_spec=pltpu.PrefetchScalarGridSpec(
            num_scalar_prefetch=1,
            grid=(n_ctx,),
            in_specs=[vmem] * (2 * n_ctx - 1)
            + [pl.BlockSpec((1, cols, feats), lambda g, s: (s[2 + n_ctx + g], 0, 0))],
            out_specs=[pl.BlockSpec((1, cols, total), lambda g, s: (g, 0, 0))] * 2,
            scratch_shapes=[pltpu.VMEM((2, total, feats), jnp.bfloat16)],
        ),
        out_shape=[
            jax.ShapeDtypeStruct((n_ctx, cols, total), jnp.bfloat16),
            jax.ShapeDtypeStruct((n_ctx, cols, total), jnp.float32),
        ],
        name="project",
    )(scal, x, *mine, *theirs, w_t)


def rot_t(v, cos, sin):
    half = v.shape[0] // 2
    v1, v2 = v[:half], v[half:]
    return jnp.concatenate([v1 * cos - v2 * sin, v2 * cos + v1 * sin], axis=0)


def gather_kernel(n_ctx, scal, *refs):
    pieces, (cos, sin, q_ref, kv_ref, whole) = refs[:n_ctx], refs[n_ctx:]
    cols = pieces[0].shape[0]
    for k in range(n_ctx):
        at = pl.ds(pl.multiple_of(scal[2 + n_ctx + k] * cols, 16), cols)
        whole[at, :] = pieces[k][...]
    q_rows = G * HD
    q_ref[...] = whole[:q_rows, :]
    key = whole[q_rows : q_rows + HD, :].astype(jnp.float32)
    kv_ref[:HD, :] = rot_t(key, cos[...], sin[...]).astype(jnp.bfloat16)
    kv_ref[HD:, :] = whole[q_rows + HD :, :]


def gather_head(scal, pieces, cos, sin):
    n_ctx = len(pieces)
    cols, total = pieces[0].shape
    return pl.pallas_call(
        functools.partial(gather_kernel, n_ctx),
        in_specs=[pl.BlockSpec(memory_space=pltpu.SMEM)] + [vmem] * (n_ctx + 2),
        out_specs=[vmem, vmem],
        out_shape=[
            jax.ShapeDtypeStruct((G * HD, total), jnp.bfloat16),
            jax.ShapeDtypeStruct((2 * HD, total), jnp.bfloat16),
        ],
        scratch_shapes=[pltpu.VMEM((n_ctx * cols, total), jnp.bfloat16)],
        name="gather_head",
    )(scal, *pieces, cos, sin)


def attend_kernel(n_ctx, rows, scal, q_ref, kv_ref, kvo_ref, old_ref, ci, si, cs, ss, cn, sn, *refs):
    outs, ho = refs[:n_ctx], refs[n_ctx]
    me_sub = scal[0]
    total = n_ctx * rows
    part = total // 2
    scale = HD ** (-0.5)
    half_blocks = n_ctx // 2
    span = half_blocks * 2 * rows

    def queries(cos, sin, lanes):
        c, s = cos[:, lanes], sin[:, lanes]
        done = []
        for g in range(G):
            v = q_ref[g * HD : (g + 1) * HD, lanes].astype(jnp.float32)
            done.append(rot_t(v, c, s).astype(jnp.bfloat16))
        return jnp.concatenate(done, axis=1)

    def place(index, sub):
        return (index // rows) * (2 * rows) + sub * rows + index % rows

    def tr(v):
        return jnp.transpose(v.astype(jnp.float32)).astype(jnp.bfloat16)

    def old_span(a, lo):
        blocks = old_ref[:, a * half_blocks : (a + 1) * half_blocks]
        return blocks.reshape(2 * half_blocks * rows, 2 * HD)[:, lo : lo + HD]

    key_i = lax.broadcasted_iota(jnp.int32, (part, part), 0)
    row_i = lax.broadcasted_iota(jnp.int32, (part, part), 1)
    row_p = place(row_i, me_sub)
    keep_own = place(key_i, me_sub) <= row_p
    keep_other = place(key_i, 1 - me_sub) <= row_p
    keep = jnp.concatenate([keep_own, keep_other], axis=0)
    keep = jnp.concatenate([keep] * G, axis=1)

    def cur_keys(b):
        lanes = slice(b * part, (b + 1) * part)
        return jnp.concatenate([tr(kv_ref[:HD, lanes]), tr(kvo_ref[:HD, lanes])], axis=0)

    def cur_vals(b):
        lanes = slice(b * part, (b + 1) * part)
        return jnp.concatenate([kv_ref[HD:, lanes], kvo_ref[HD:, lanes]], axis=1)

    old_v = [tr(old_span(a, HD)) for a in range(2)]
    keys_cur = [cur_keys(0), None]
    keys_cur[1] = cur_keys(1)
    vals_cur = [cur_vals(0), cur_vals(1)]
    for b in range(2):
        lanes = slice(b * part, (b + 1) * part)
        q_intra = queries(ci, si, lanes)
        q_succ = queries(cs, ss, lanes)
        q_inter = queries(cn, sn, lanes)
        jobs = [(old_span(0, 0), q_inter, old_v[0], False)]
        jobs.append((old_span(1, 0), q_succ if b == 0 else q_inter, old_v[1], False))
        if b == 1:
            jobs.append((keys_cur[0], q_succ, vals_cur[0], False))
        jobs.append((keys_cur[b], q_intra, vals_cur[b], True))
        scores = []
        for key, query, _, masked in jobs:
            sc = dot32(key, query, ((1,), (0,)))
            if masked:
                sc = jnp.where(keep, sc, neg_big)
            scores.append(sc)
        top = scores[0].max(axis=0, keepdims=True)
        for sc in scores[1:]:
            top = jnp.maximum(top, sc.max(axis=0, keepdims=True))
        acc = None
        weight_sum = None
        for sc, (_, _, val, masked) in zip(scores, jobs):
            w = jnp.exp((sc - top) * scale)
            ws = w.sum(axis=0, keepdims=True)
            o = dot32(val, w.astype(jnp.bfloat16), ((1,), (0,)))
            acc = o if acc is None else acc + o
            weight_sum = ws if weight_sum is None else weight_sum + ws
        res = (acc / weight_sum).astype(jnp.bfloat16)
        for g in range(G):
            ho[g * HD : (g + 1) * HD, lanes] = res[:, g * part : (g + 1) * part]
    chunk = outs[0].shape[0]
    for k in range(n_ctx):
        at = pl.ds(pl.multiple_of(scal[2 + n_ctx + k] * chunk, 16), chunk)
        outs[k][...] = ho[at, :]


def attend(scal, q, kv, kvo, old, tables):
    n_ctx, rows = old.shape[1], old.shape[2]
    total = n_ctx * rows
    chunk = G * HD // n_ctx
    return pl.pallas_call(
        functools.partial(attend_kernel, n_ctx, rows),
        in_specs=[pl.BlockSpec(memory_space=pltpu.SMEM)] + [vmem] * 10,
        out_specs=[vmem] * n_ctx,
        out_shape=[jax.ShapeDtypeStruct((chunk, total), jnp.bfloat16)] * n_ctx,
        scratch_shapes=[pltpu.VMEM((G * HD, total), jnp.bfloat16)],
        name="attend",
    )(scal, q, kv, kvo, old, *tables)


def arrange_kernel(n_ctx, rows, scal, *refs):
    pieces, (a_ref, at_s, a_s) = refs[:n_ctx], refs[n_ctx:]
    chunk = pieces[0].shape[0]
    for k in range(n_ctx):
        at = pl.ds(pl.multiple_of(scal[2 + n_ctx + k] * chunk, 16), chunk)
        at_s[at, :] = pieces[k][...]
    a_s[...] = jnp.transpose(at_s[...].astype(jnp.float32)).astype(jnp.bfloat16)
    for k in range(n_ctx):
        at = pl.ds(pl.multiple_of(scal[2 + k] * rows, rows), rows)
        a_ref[k * rows : (k + 1) * rows, :] = a_s[at, :]


def arrange(scal, pieces):
    n_ctx = len(pieces)
    chunk, total = pieces[0].shape
    return pl.pallas_call(
        functools.partial(arrange_kernel, n_ctx, total // n_ctx),
        in_specs=[pl.BlockSpec(memory_space=pltpu.SMEM)] + [vmem] * n_ctx,
        out_specs=vmem,
        out_shape=jax.ShapeDtypeStruct((total, n_ctx * chunk), jnp.bfloat16),
        scratch_shapes=[
            pltpu.VMEM((n_ctx * chunk, total), jnp.bfloat16),
            pltpu.VMEM((total, n_ctx * chunk), jnp.bfloat16),
        ],
        name="arrange",
    )(scal, *pieces)


def out_kernel(n_ctx, rows, first, a_ref, w_ref, *outs):
    w = w_ref[...].reshape(w_ref.shape[0] * w_ref.shape[1], w_ref.shape[2])
    res = dot32(a_ref[...], w, ((1,), (0,)))
    for k in range(n_ctx):
        outs[k][...] = res[k * rows : (k + 1) * rows].astype(outs[k].dtype)


def out_half(first, a, w_out, n_ctx, n_head, dtype):
    total = a.shape[0]
    rows = total // n_ctx
    width = w_out.shape[2] // n_head
    tile = 512
    steps = width // tile
    return pl.pallas_call(
        functools.partial(out_kernel, n_ctx, rows),
        grid_spec=pltpu.PrefetchScalarGridSpec(
            num_scalar_prefetch=1,
            grid=(steps,),
            in_specs=[
                vmem,
                pl.BlockSpec(
                    (w_out.shape[0], w_out.shape[1], tile), lambda g, f: (0, 0, f[0] * steps + g)
                ),
            ],
            out_specs=[pl.BlockSpec((rows, tile), lambda g, f: (0, g))] * n_ctx,
        ),
        out_shape=[jax.ShapeDtypeStruct((rows, width), dtype)] * n_ctx,
        name="out_half",
    )(first, a, w_out)


def local_fast(hidden_in, w_qkv, qkv_bias, w_out, prev_keys, prev_values, shard_blocks):
    n_ctx = lax.axis_size("ctx")
    n_head = lax.axis_size("head")
    tok_ctx = hidden_in.shape[0]
    rows = tok_ctx // 2
    span_len = rows * n_ctx
    me_ctx = lax.axis_index("ctx")
    me_sub = lax.axis_index("sub")
    me_head = lax.axis_index("head")
    order = me_ctx ^ jnp.arange(n_ctx, dtype=jnp.int32)
    blocks = lookup(shard_blocks, order)
    slot = jnp.where(me_head == me_sub, 0, 1)
    scal = jnp.concatenate(
        [jnp.stack([me_sub, slot]).astype(jnp.int32), blocks.astype(jnp.int32), order]
    )

    own_rows = lax.dynamic_slice_in_dim(hidden_in, me_head * rows, rows, 0)
    mine = [flip(own_rows, "ctx", k) for k in range(1, n_ctx)]
    theirs = [flip(m, "head", 1) for m in mine]

    old_pos = ((me_ctx * 2 + me_sub) * rows + jnp.arange(rows, dtype=jnp.int32)) % span_len
    k_prev = rotate(prev_keys.astype(jnp.float32), old_pos).astype(jnp.bfloat16)
    old_local = jnp.transpose(jnp.concatenate([k_prev, prev_values], axis=-1), (1, 0, 2))
    old_pieces = [
        lax.dynamic_index_in_dim(old_local, order[k], 0, keepdims=False) for k in range(n_ctx)
    ]
    old_pieces = [old_pieces[0]] + [flip(old_pieces[k], "ctx", k) for k in range(1, n_ctx)]
    old_stack = jnp.stack(old_pieces)
    old_stack = jnp.stack(
        [
            lax.dynamic_index_in_dim(old_stack, me_ctx ^ c, 0, keepdims=False)
            for c in range(n_ctx)
        ]
    )
    old = jnp.stack([old_stack, flip(old_stack, "sub", 1)])

    half = HD // 2
    frequency = rope_base ** (-(jnp.arange(half, dtype=jnp.float32) * 2.0) / HD)
    lane = jnp.arange(n_ctx * rows, dtype=jnp.int32)
    local_pos = ((lane // rows) * tok_ctx + me_sub * rows + lane % rows) % span_len

    def table(pos):
        angle = frequency[:, None] * pos.astype(jnp.float32)[None, :]
        return jnp.cos(angle), jnp.sin(angle)

    intra = table(local_pos)
    succ = table(local_pos + span_len)
    inter = table(jnp.full_like(local_pos, 2 * span_len - 1))

    w_t = jnp.transpose(w_qkv, (1, 2, 0))
    cols = w_t.shape[1]
    send, own = project(scal, hidden_in, mine, theirs, w_t)
    got = flip(send, "sub", 1)
    bias = lax.dynamic_slice_in_dim(qkv_bias, me_ctx * cols, cols, 1).astype(jnp.float32)
    bias = jnp.stack(
        [lax.dynamic_index_in_dim(bias, order[k], 0, keepdims=False) for k in range(n_ctx)]
    )
    joined = [
        (own[k] + got[k].astype(jnp.float32) + bias[k][:, None]).astype(jnp.bfloat16)
        for k in range(n_ctx)
    ]
    pieces = [joined[0]] + [flip(joined[k], "ctx", k) for k in range(1, n_ctx)]
    q, kv = gather_head(scal, pieces, *intra)
    kvo = flip(kv, "sub", 1)
    heads = attend(scal, q, kv, kvo, old, (*intra, *succ, *inter))
    pieces = [heads[0]] + [flip(heads[k], "ctx", k) for k in range(1, n_ctx)]
    a = arrange(scal, pieces)
    away = out_half(jnp.reshape(1 - me_head, (1,)), a, w_out, n_ctx, n_head, jnp.bfloat16)
    home = out_half(jnp.reshape(me_head, (1,)), a, w_out, n_ctx, n_head, jnp.float32)
    total = None
    for k in range(n_ctx - 1, -1, -1):
        term = home[k] + flip(away[k], "head", 1).astype(jnp.float32)
        if k:
            term = flip(term.astype(jnp.bfloat16), "ctx", k).astype(jnp.float32)
        total = term if total is None else total + term
    return total.astype(jnp.bfloat16)


def local(hidden_in, w_qkv, qkv_bias, w_out, prev_keys, prev_values, shard_blocks):
    n_ctx = lax.axis_size("ctx")
    n_sub = lax.axis_size("sub")
    n_head = lax.axis_size("head")
    tok_ctx = hidden_in.shape[0]
    tok_dev = tok_ctx // n_sub
    span_len = tok_ctx * n_ctx // 2
    kv_dev = w_qkv.shape[1]
    me_ctx = lax.axis_index("ctx")
    me_sub = lax.axis_index("sub")
    partial_value = jnp.einsum(
        "td,dhn->thn",
        hidden_in,
        lax.all_gather(w_qkv, "ctx", axis=2, tiled=True),
        preferred_element_type=jnp.float32,
    )
    joined = lax.psum_scatter(partial_value, "sub", scatter_dimension=0, tiled=True)
    joined = (joined + qkv_bias.astype(jnp.float32)[None]).reshape(tok_dev, kv_dev, G + 2, HD)
    owner_block = lookup(shard_blocks, me_ctx)
    positions = owner_block * tok_ctx + me_sub * tok_dev + jnp.arange(tok_dev, dtype=jnp.int32)
    span_q = NPREV + positions // span_len
    local_q = positions % span_len
    queries = joined[:, :, :G]

    def arrange(rotated):
        return jnp.transpose(rotated.astype(jnp.bfloat16), (1, 0, 2, 3)).reshape(
            kv_dev, tok_dev * G, HD
        )

    q_intra = arrange(rotate(queries, local_q))
    q_succ = arrange(rotate(queries, local_q + span_len))
    q_inter = arrange(rotate(queries, jnp.full((tok_dev,), 2 * span_len - 1, jnp.int32)))
    k_cur = rotate(joined[:, :, G], local_q).astype(jnp.bfloat16)
    v_cur = joined[:, :, G + 1].astype(jnp.bfloat16)
    old_rows = (me_ctx * n_sub + me_sub) * tok_dev + jnp.arange(tok_dev, dtype=jnp.int32)
    k_prev = rotate(prev_keys.astype(jnp.float32), old_rows % span_len).astype(jnp.bfloat16)
    row_span = jnp.repeat(span_q, G)
    row_local = jnp.repeat(local_q, G)
    own_span = span_q[0]
    score_scale = HD ** (-0.5)
    row_count = tok_dev * G
    start_state = (
        jnp.full((kv_dev, row_count), neg_big, jnp.float32),
        jnp.zeros((kv_dev, row_count), jnp.float32),
        jnp.zeros((kv_dev, row_count, HD), jnp.float32),
    )

    def scores_of(query_set, key_block):
        return (
            jnp.einsum("hrd,khd->hrk", query_set, key_block, preferred_element_type=jnp.float32)
            * score_scale
        )

    def update(running, scores, allowed, value_block):
        running_max, weight_sum, weighted = running
        block_max = jnp.max(jnp.where(allowed, scores, neg_big), axis=2)
        new_max = jnp.maximum(running_max, block_max)
        weights = jnp.where(allowed, jnp.exp(scores - new_max[..., None]), 0.0)
        rescale = jnp.exp(running_max - new_max)
        weight_sum = weight_sum * rescale + jnp.sum(weights, axis=2)
        weighted = weighted * rescale[..., None] + jnp.einsum(
            "hrk,khd->hrd",
            weights.astype(jnp.bfloat16),
            value_block,
            preferred_element_type=jnp.float32,
        )
        return (new_max, weight_sum, weighted)

    def current_block(running, key_block, value_block, key_index):
        shard_index = key_index // tok_dev
        key_pos = (
            lookup(shard_blocks, shard_index // n_sub) * tok_ctx
            + shard_index % n_sub * tok_dev
            + key_index % tok_dev
        )
        key_span = NPREV + key_pos // span_len
        key_local = key_pos % span_len
        same_span = key_span[None, :] == row_span[:, None]
        before = key_span[None, :] == row_span[:, None] - 1
        allowed = same_span & (key_local[None, :] <= row_local[:, None]) | before
        query_set = jnp.where(key_span[0] == own_span, q_intra, q_succ)
        return update(running, scores_of(query_set, key_block), allowed[None], value_block)

    def earlier_block(running, key_block, value_block, key_index):
        block_span = key_index[0] // span_len
        query_set = jnp.where(block_span == own_span - 1, q_succ, q_inter)
        scores = scores_of(query_set, key_block)
        return update(running, scores, jnp.ones(scores.shape, jnp.bool_), value_block)

    cur_keys = lax.all_gather(k_cur, ("ctx", "sub"), axis=0, tiled=True)
    cur_values = lax.all_gather(v_cur, ("ctx", "sub"), axis=0, tiled=True)
    old_keys = lax.all_gather(k_prev, ("ctx", "sub"), axis=0, tiled=True)
    old_values = lax.all_gather(prev_values, ("ctx", "sub"), axis=0, tiled=True)
    piece_rows = cur_keys.shape[0]
    block_rows = math.gcd(piece_rows, tok_dev)

    def turn(turn_index, state_in):
        offset = turn_index * block_rows
        key_index = offset + jnp.arange(block_rows, dtype=jnp.int32)

        def take(values):
            return lax.dynamic_slice_in_dim(values, offset, block_rows, 0)

        state_in = current_block(state_in, take(cur_keys), take(cur_values), key_index)
        return earlier_block(state_in, take(old_keys), take(old_values), key_index)

    running_max, weight_sum, weighted = lax.fori_loop(
        0, piece_rows // block_rows, turn, start_state
    )
    head_out = (weighted / weight_sum[..., None]).astype(jnp.bfloat16)
    head_out = jnp.transpose(head_out.reshape(kv_dev, tok_dev, G, HD), (1, 0, 2, 3)).reshape(
        tok_dev, kv_dev, G * HD
    )
    group_cols = w_out.shape[2] // (n_head * n_sub)
    split_cols = w_out.reshape(kv_dev, w_out.shape[1], n_head, n_sub, group_cols)
    own_cols = lax.dynamic_index_in_dim(split_cols, me_sub, 3, keepdims=False).reshape(
        kv_dev, w_out.shape[1], n_head * group_cols
    )
    pair_heads = lax.all_gather(head_out, "sub", axis=0, tiled=True)
    summed = jnp.einsum(
        "thn,hnd->td",
        pair_heads,
        lax.all_gather(own_cols, "ctx", axis=1, tiled=True),
        preferred_element_type=jnp.float32,
    )
    shares = lax.psum_scatter(summed.astype(jnp.bfloat16), "head", scatter_dimension=1, tiled=True)
    return lax.all_to_all(shares, "sub", split_axis=0, concat_axis=1, tiled=True)


def one_head_per_ctx(mesh, w_qkv):
    n_ctx, n_head, n_sub = mesh.shape["ctx"], mesh.shape["head"], mesh.shape["sub"]
    return (
        n_head == 2
        and n_sub == 2
        and n_ctx & (n_ctx - 1) == 0
        and n_ctx > 1
        and w_qkv.shape[1] == n_head * n_ctx
    )


def solution(mesh):
    def run(*args):
        body = local_fast if one_head_per_ctx(mesh, args[1]) else local
        return jax.shard_map(
            body,
            mesh=mesh,
            in_specs=(
                P(("groups", "ctx"), "sub"),
                P("sub", "head", "ctx"),
                P("head", None),
                P("head", "ctx", None),
                P(("groups", "ctx", "sub"), "head", None),
                P(("groups", "ctx", "sub"), "head", None),
                P("groups"),
            ),
            out_specs=P(("groups", "ctx", "sub"), "head"),
            check_vma=False,
        )(*args)

    return run
```
